32 devices in a mesh: shard: 2 (over y), ctx: 4 (over x, core), tp: 4 (over z).
Axes of the slice: x: 2, y: 2, z: 4, core: 2. Of those that a mesh axis runs over, the one named last changes fastest.
Arguments:
- image_tokens: bfloat16 [4, 1024, 1536], P('shard', 'ctx', 'tp'), may hold values from -6 to 6
- text_tokens: bfloat16 [4, 256, 1536], P('shard', 'ctx', 'tp'), may hold values from -6 to 6
- conditioning: bfloat16 [4, 1536], replicated, may hold values from -16 to 16
- seq_table: int32 [4], replicated, may hold values from 0 to 3, each once
- image_len: int32 [4], replicated, may hold values from 256 to 1024, as said below
- text_len: int32 [4], replicated, may hold values from 38 to 154, as said below
- mod_weight: bfloat16 [2, 1536, 6, 1536], P(None, ('shard', 'ctx', 'tp')), may hold values from -0.15625 to 0.15625
- mod_bias: bfloat16 [2, 6, 1536], P(None, None, ('shard', 'ctx', 'tp')), may hold values from -3 to 3
- qkv_weight: bfloat16 [2, 1536, 3, 1536], P(None, ('shard', 'ctx'), None, 'tp'), may hold values from -0.15625 to 0.15625
- qkv_bias: bfloat16 [2, 2, 24, 64], P(None, None, 'tp', ('shard', 'ctx')), may hold values from -1.1953125 to 1.1953125
- out_weight: bfloat16 [2, 1536, 1536], P(None, ('shard', 'ctx'), 'tp'), may hold values from -0.75 to 0.75
- out_bias: bfloat16 [2, 24, 64], P(None, 'tp', ('shard', 'ctx')), may hold values from -3 to 3
- fc1_weight: bfloat16 [2, 1536, 6144], P(None, ('shard', 'ctx'), 'tp'), may hold values from -0.15625 to 0.15625
- fc1_bias: bfloat16 [2, 96, 64], P(None, 'tp', ('shard', 'ctx')), may hold values from -3 to 3
- fc2_weight: bfloat16 [2, 1536, 6144], P(None, ('shard', 'ctx'), 'tp'), may hold values from -0.078125 to 0.078125
- fc2_bias: bfloat16 [2, 24, 64], P(None, 'tp', ('shard', 'ctx')), may hold values from -3 to 3
- image_cot: bfloat16 [4, 1024, 1536], P('shard', 'ctx', 'tp'), may hold values from -6 to 6
- text_cot: bfloat16 [4, 256, 1536], P('shard', 'ctx', 'tp'), may hold values from -6 to 6
Outputs:
- image_out: bfloat16 [4, 1024, 1536], P('shard', 'ctx', 'tp')
- text_out: bfloat16 [4, 256, 1536], P('shard', 'ctx', 'tp')
- image_grad: float32 [4, 1024, 1536], P('shard', 'ctx', 'tp')
- text_grad: float32 [4, 256, 1536], P('shard', 'ctx', 'tp')
- cond_grad: float32 [4, 1536], P(None, ('shard', 'ctx', 'tp'))
- mod_weight_grad: float32 [2, 1536, 6, 1536], P(None, ('shard', 'ctx', 'tp'))
- mod_bias_grad: float32 [2, 6, 1536], P(None, None, ('shard', 'ctx', 'tp'))
- qkv_weight_grad: float32 [2, 1536, 3, 1536], P(None, ('shard', 'ctx'), None, 'tp')
- qkv_bias_grad: float32 [2, 2, 24, 64], P(None, None, 'tp', ('shard', 'ctx'))
- out_weight_grad: float32 [2, 1536, 1536], P(None, ('shard', 'ctx'), 'tp')
- out_bias_grad: float32 [2, 24, 64], P(None, 'tp', ('shard', 'ctx'))
- fc1_weight_grad: float32 [2, 1536, 6144], P(None, ('shard', 'ctx'), 'tp')
- fc1_bias_grad: float32 [2, 96, 64], P(None, 'tp', ('shard', 'ctx'))
- fc2_weight_grad: float32 [2, 1536, 6144], P(None, ('shard', 'ctx'), 'tp')
- fc2_bias_grad: float32 [2, 24, 64], P(None, 'tp', ('shard', 'ctx'))
The draws below stay inside these ranges and needn't reach their ends.
Inputs may be any that keep to these rules, and one draw needn't show every extreme that they name: Slot s takes conditioning row seq_table[s]; every row is taken once. `image_len`: some slot has all 1024 image tokens valid in every draw. `text_len`: some slot has 154 valid text tokens in every draw; text slots from 154 on are never valid.
All inputs are finite; a program needn't handle non-finite values.
Results may differ from the reference program's by a relative error of at most 0.014.
The reference program's roundings to bfloat16 on the way count: a program that leaves them out, or rounds other values in their place, can miss the bound.
Values may be sent and summed in bfloat16 or wider, within the bound.
No kernel may reach another device: no remote copies, remote signals or barrier semaphores. Data moves between devices by JAX's collectives and lax.ppermute only.
A program may use at most 256 MiB of HBM per device.

```python
import math
import jax
import jax.numpy as jnp
from jax import lax

D = 1536
HEADS = 24
HD = 64
FF = 6144
LI = 1024
LT = 256
TXT = 154
SEQS = 4


def draw_conditioning(key, part):
    base = jax.random.normal(key, (SEQS, D), jnp.float32)
    return jnp.clip(base, -16.0, 16.0).astype(jnp.bfloat16)


def draw_image_len(key, part):
    counts = jax.random.randint(key, (SEQS,), LI // 4, LI + 1)
    full_slot = jax.random.randint(jax.random.fold_in(key, 3), (), 0, SEQS)
    return counts.at[full_slot].set(LI).astype(jnp.int32)


def draw_text_len(key, part):
    counts = jax.random.randint(key, (SEQS,), TXT // 4, TXT + 1)
    full_slot = jax.random.randint(jax.random.fold_in(key, 5), (), 0, SEQS)
    return counts.at[full_slot].set(TXT).astype(jnp.int32)


def block_levels(own_key, dims, cuts, least, largest):
    factor_of, own = 1.0, jax.random.fold_in(own_key, 6)
    for axis_at, blocks in cuts:
        draws = jnp.exp(jax.random.uniform(jax.random.fold_in(own, axis_at), (blocks,), jnp.float32, least / len(cuts), largest / len(cuts)))
        factor_of = factor_of * jnp.repeat(draws, dims[axis_at] // blocks).reshape([-1 if axis == axis_at else 1 for axis in range(len(dims))])
    return factor_of


def normal_values(key, extent, spread, most, shards=(), held_as=jnp.bfloat16):
    drawn = spread * jax.random.normal(key, extent, jnp.float32)
    if shards:
        drawn = drawn * block_levels(key, extent, shards, -0.22, 0.18)
    return jnp.clip(drawn, -most, most).astype(held_as)


def setup_inputs(seed: int = 0) -> dict:
    splits = jax.random.split(jax.random.key(seed), 19)
    return {
        "image_tokens": normal_values(splits[0], (SEQS, LI, D), 1.0, 6.0, ((0, 2), (1, 4), (2, 4))),
        "text_tokens": normal_values(splits[1], (SEQS, LT, D), 1.0, 6.0, ((0, 2), (1, 4), (2, 4))),
        "conditioning": draw_conditioning(jax.random.fold_in(splits[18], 71), 0),
        "seq_table": jax.random.permutation(splits[3], SEQS).astype(jnp.int32),
        "image_len": draw_image_len(jax.random.fold_in(splits[18], 71), 0),
        "text_len": draw_text_len(jax.random.fold_in(splits[18], 71), 0),
        "mod_weight": normal_values(splits[6], (2, D, 6, D), D ** -0.5, 0.15625, ((1, 32),)),
        "mod_bias": normal_values(splits[7], (2, 6, D), 0.5, 3.0, ((2, 32),)),
        "qkv_weight": normal_values(splits[8], (2, D, 3, D), D ** -0.5, 0.15625, ((1, 8), (3, 4))),
        "qkv_bias": normal_values(splits[9], (2, 2, HEADS, HD), 0.2, 1.1953125, ((2, 4), (3, 8))),
        "out_weight": normal_values(splits[10], (2, D, D), HD ** -0.5, 0.75, ((1, 8), (2, 4))),
        "out_bias": normal_values(splits[11], (2, HEADS, HD), 0.5, 3.0, ((1, 4), (2, 8))),
        "fc1_weight": normal_values(splits[12], (2, D, FF), D ** -0.5, 0.15625, ((1, 8), (2, 4))),
        "fc1_bias": normal_values(splits[13], (2, FF // HD, HD), 0.5, 3.0, ((1, 4), (2, 8))),
        "fc2_weight": normal_values(splits[14], (2, D, FF), FF ** -0.5, 0.078125, ((1, 8), (2, 4))),
        "fc2_bias": normal_values(splits[15], (2, HEADS, HD), 0.5, 3.0, ((1, 4), (2, 8))),
        "image_cot": normal_values(splits[16], (SEQS, LI, D), 1.0, 6.0, ((0, 2), (1, 4), (2, 4))),
        "text_cot": normal_values(splits[17], (SEQS, LT, D), 1.0, 6.0, ((0, 2), (1, 4), (2, 4))),
    }


EPSILON = 1e-06
NEG_LARGE = -1e+30
GELU_COEF = math.sqrt(2.0 / math.pi)
PRECISE = lax.Precision.HIGHEST

def layer_norm(values):
    center = values - lax.optimization_barrier(jnp.mean(values, -1, keepdims=True))
    inv_std = lax.rsqrt(lax.optimization_barrier(jnp.mean(center * center, -1, keepdims=True)) + EPSILON)
    return (center * inv_std, inv_std)

def norm_back(normed, inv_std, grad_in):
    return inv_std * (grad_in - lax.optimization_barrier(jnp.mean(grad_in, -1, keepdims=True)) - normed * lax.optimization_barrier(jnp.mean(grad_in * normed, -1, keepdims=True)))

def gelu_tanh(values):
    return 0.5 * values * (1.0 + jnp.tanh(GELU_COEF * (values + 0.044715 * values * values * values)))

def gelu_slope(values):
    tanh_val = jnp.tanh(GELU_COEF * (values + 0.044715 * values * values * values))
    return 0.5 * (1.0 + tanh_val) + 0.5 * values * (1.0 - tanh_val * tanh_val) * GELU_COEF * (1.0 + 0.134145 * values * values)

def silu_slope(values):
    sigmoid = jax.nn.sigmoid(values)
    return sigmoid * (1.0 + values * (1.0 - sigmoid))

def round_half(values):
    return lax.optimization_barrier(values.astype(jnp.bfloat16)).astype(jnp.float32)

def split_heads(packed):
    return packed.reshape(packed.shape[0], 3, -1, HD).astype(jnp.float32)

def joint_scores(head_parts, key_valid, score_scale):
    scores = jnp.einsum('qhd,khd->hqk', head_parts[:, 0], head_parts[:, 1]) * score_scale
    return jnp.where(key_valid[None, None, :], scores, NEG_LARGE)

def attend(packed, key_valid, score_scale):
    head_parts = split_heads(packed)
    scores = joint_scores(head_parts, key_valid, score_scale)
    top_score = lax.optimization_barrier(jnp.max(scores, -1, keepdims=True))
    log_total = top_score + jnp.log(lax.optimization_barrier(jnp.sum(jnp.exp(scores - top_score), -1, keepdims=True)))
    weights = round_half(jnp.exp(scores - log_total))
    mixed = jnp.einsum('hqk,khd->qhd', weights, head_parts[:, 2]).astype(jnp.bfloat16)
    return (mixed.reshape(packed.shape[0], -1), log_total)

def attend_back(packed, key_valid, mixed, log_total, grad_mixed, score_scale):
    length = packed.shape[0]
    head_parts = split_heads(packed)
    mixed_rows = mixed.reshape(length, -1, HD).astype(jnp.float32)
    grad_rows = grad_mixed.reshape(length, -1, HD).astype(jnp.float32)
    prob_rows = jnp.exp(joint_scores(head_parts, key_valid, score_scale) - log_total)
    grad_prob = jnp.einsum('qhd,khd->hqk', grad_rows, head_parts[:, 2])
    row_delta = jnp.transpose(lax.optimization_barrier(jnp.sum(grad_rows * mixed_rows, -1)))
    grad_scores = round_half(prob_rows * (grad_prob - row_delta[:, :, None]) * score_scale)
    grad_query = jnp.einsum('hqk,khd->qhd', grad_scores, head_parts[:, 1])
    grad_key = jnp.einsum('hqk,qhd->khd', grad_scores, head_parts[:, 0])
    grad_value = jnp.einsum('hqk,qhd->khd', round_half(prob_rows), grad_rows)
    stacked = jnp.stack([grad_query, grad_key, grad_value], 1)
    return stacked.reshape(length, 3, -1).astype(jnp.bfloat16)

def reference(image_tokens, text_tokens, conditioning, seq_table, image_len, text_len, mod_weight, mod_bias, qkv_weight, qkv_bias, out_weight, out_bias, fc1_weight, fc1_bias, fc2_weight, fc2_bias, image_cot, text_cot):
    score_scale = 1.0 / math.sqrt(HD)
    cond_rows = jnp.take(conditioning, seq_table, axis=0).astype(jnp.float32)
    cond_act = jax.nn.silu(cond_rows)
    mod_full = mod_weight.astype(jnp.float32)
    modulation = jnp.einsum('sd,xdke->sxke', cond_act, mod_full, precision=PRECISE) + mod_bias.astype(jnp.float32)[None]
    w_qkv = qkv_weight.astype(jnp.float32)
    w_out = out_weight.astype(jnp.float32)
    w_fc1 = fc1_weight.astype(jnp.float32)
    w_fc2 = fc2_weight.astype(jnp.float32)
    b_qkv = qkv_bias.astype(jnp.float32).reshape(2, 2, D)
    bias_three = jnp.stack([b_qkv[:, 0], jnp.zeros((2, D), jnp.float32), b_qkv[:, 1]], 1)
    b_out = out_bias.astype(jnp.float32).reshape(2, D)
    b_fc1 = fc1_bias.astype(jnp.float32).reshape(2, FF)
    b_fc2 = fc2_bias.astype(jnp.float32).reshape(2, D)

    def one_sequence(totals, item):
        inputs = (item[0], item[1])
        cots = (item[2], item[3])
        mod_rows = item[4]
        key_valid = jnp.concatenate([jnp.arange(LI) < item[5], jnp.arange(LT) < item[6]])
        normed_one, inv_one, hidden_one, packed = ([], [], [], [])
        for stream in range(2):
            normed, inv_std = layer_norm(inputs[stream].astype(jnp.float32))
            hidden = (normed * (1.0 + mod_rows[stream, 1]) + mod_rows[stream, 0]).astype(jnp.bfloat16)
            projected = jnp.einsum('nd,dkh->nkh', hidden.astype(jnp.float32), w_qkv[stream]) + bias_three[stream]
            normed_one.append(normed)
            inv_one.append(inv_std)
            hidden_one.append(hidden)
            packed.append(projected.astype(jnp.bfloat16))
        joint = jnp.concatenate(packed, 0)
        mixed, log_total = attend(joint, key_valid, score_scale)
        mixed_tok = (mixed[:LI], mixed[LI:])
        outputs, grad_resid, grad_mixed, grads_rest, mod_rest = ([], [], [], [], [])
        for stream in range(2):
            mods = mod_rows[stream]
            mixed_f = mixed_tok[stream].astype(jnp.float32)
            branch_one = jnp.einsum('nh,oh->no', mixed_f, w_out[stream]) + b_out[stream]
            resid = inputs[stream].astype(jnp.float32) + mods[2] * branch_one
            normed_two, inv_two = layer_norm(resid)
            hidden_two = (normed_two * (1.0 + mods[4]) + mods[3]).astype(jnp.bfloat16)
            pre_act = jnp.einsum('nd,df->nf', hidden_two.astype(jnp.float32), w_fc1[stream]) + b_fc1[stream]
            act_two = gelu_tanh(pre_act).astype(jnp.bfloat16)
            branch_two = jnp.einsum('nf,of->no', act_two.astype(jnp.float32), w_fc2[stream]) + b_fc2[stream]
            outputs.append((resid + mods[5] * branch_two).astype(jnp.bfloat16))
            cot_f = cots[stream].astype(jnp.float32)
            grad_two = cot_f * mods[5]
            grad_two_half = round_half(grad_two)
            fc2_grad = jnp.einsum('no,nf->of', grad_two_half, act_two.astype(jnp.float32))
            grad_act = jnp.einsum('no,of->nf', grad_two_half, w_fc2[stream]) * gelu_slope(pre_act)
            grad_act_half = round_half(grad_act)
            fc1_grad = jnp.einsum('nd,nf->df', hidden_two.astype(jnp.float32), grad_act_half)
            grad_hidden_two = jnp.einsum('nf,df->nd', grad_act_half, w_fc1[stream])
            grad_res = cot_f + norm_back(normed_two, inv_two, grad_hidden_two * (1.0 + mods[4]))
            grad_one = grad_res * mods[2]
            grad_one_half = round_half(grad_one)
            out_grad = jnp.einsum('no,nh->oh', grad_one_half, mixed_f)
            grad_mixed.append(jnp.einsum('no,oh->nh', grad_one_half, w_out[stream]).astype(jnp.bfloat16))
            grad_resid.append(grad_res)
            grads_rest.append((out_grad, lax.optimization_barrier(jnp.sum(grad_one, 0)), fc1_grad, lax.optimization_barrier(jnp.sum(grad_act, 0)), fc2_grad, lax.optimization_barrier(jnp.sum(grad_two, 0))))
            mod_rest.append((lax.optimization_barrier(jnp.sum(grad_res * branch_one, 0)), lax.optimization_barrier(jnp.sum(grad_hidden_two, 0)), lax.optimization_barrier(jnp.sum(grad_hidden_two * normed_two, 0)), lax.optimization_barrier(jnp.sum(cot_f * branch_two, 0))))
        grad_joint = jnp.concatenate(grad_mixed, 0)
        grad_packed = attend_back(joint, key_valid, mixed, log_total, grad_joint, score_scale)
        grad_tok = (grad_packed[:LI], grad_packed[LI:])
        input_grads, qkv_grads, bias_grads, mod_grads = ([], [], [], [])
        for stream in range(2):
            mods = mod_rows[stream]
            grad_f = grad_tok[stream].astype(jnp.float32)
            qkv_grads.append(jnp.einsum('nd,nkh->dkh', hidden_one[stream].astype(jnp.float32), grad_f))
            bias_sum = lax.optimization_barrier(jnp.sum(grad_f, 0))
            bias_grads.append(jnp.stack([bias_sum[0], bias_sum[2]], 0))
            grad_hidden_one = jnp.einsum('nkh,dkh->nd', grad_f, w_qkv[stream])
            input_grads.append(grad_resid[stream] + norm_back(normed_one[stream], inv_one[stream], grad_hidden_one * (1.0 + mods[1])))
            gate_one, shift_two, scale_two, gate_two = mod_rest[stream]
            mod_grads.append(jnp.stack([lax.optimization_barrier(jnp.sum(grad_hidden_one, 0)), lax.optimization_barrier(jnp.sum(grad_hidden_one * normed_one[stream], 0)), gate_one, shift_two, scale_two, gate_two], 0))
        stacked = (jnp.stack(qkv_grads, 0), jnp.stack(bias_grads, 0)) + tuple((jnp.stack([grads_rest[0][which], grads_rest[1][which]], 0) for which in range(6)))
        new_totals = tuple((total + extra for total, extra in zip(totals, stacked)))
        return (new_totals, (outputs[0], outputs[1], input_grads[0], input_grads[1], jnp.stack(mod_grads, 0)))
    init = (jnp.zeros((2, D, 3, D), jnp.float32), jnp.zeros((2, 2, D), jnp.float32), jnp.zeros((2, D, D), jnp.float32), jnp.zeros((2, D), jnp.float32), jnp.zeros((2, D, FF), jnp.float32), jnp.zeros((2, FF), jnp.float32), jnp.zeros((2, D, FF), jnp.float32), jnp.zeros((2, D), jnp.float32))
    totals, per_seq = lax.scan(one_sequence, init, (image_tokens, text_tokens, image_cot, text_cot, modulation, image_len, text_len))
    image_out, text_out, image_grad, text_grad, grad_mod = per_seq
    mod_weight_grad = jnp.einsum('sd,sxke->xdke', cond_act, grad_mod, precision=PRECISE)
    mod_bias_grad = lax.optimization_barrier(jnp.sum(grad_mod, 0))
    act_grad = jnp.einsum('sxke,xdke->sd', grad_mod, mod_full, precision=PRECISE)
    cond_grad = jnp.zeros((SEQS, D), jnp.float32).at[seq_table].add(act_grad * silu_slope(cond_rows))
    return (image_out, text_out, image_grad, text_grad, cond_grad, mod_weight_grad, mod_bias_grad, totals[0], totals[1].reshape(2, 2, HEADS, HD), totals[2], totals[3].reshape(2, HEADS, HD), totals[4], totals[5].reshape(2, FF // HD, HD), totals[6], totals[7].reshape(2, HEADS, HD))
```

```python
from functools import partial
import math

import jax
import jax.numpy as jnp
from jax import lax
from jax.experimental import pallas as pl
from jax.experimental.pallas import tpu as pltpu
from jax.sharding import PartitionSpec as P

HD = 64
PAIR = 2 * HD
LI = 1024
LT = 256
SCALE = 1.0 / math.sqrt(HD)

EPSILON = 1e-06
NEG_LARGE = -1e30
GELU_COEF = math.sqrt(2.0 / math.pi)
PRECISE = lax.Precision.HIGHEST
BF = jnp.bfloat16
F32 = jnp.float32

NT = (((1,), (1,)), ((), ()))
TN = (((0,), (0,)), ((), ()))


def layer_norm(values):
    mean = jnp.mean(values, -1, keepdims=True)
    center = values - mean
    inv_std = lax.rsqrt(jnp.mean(center * center, -1, keepdims=True) + EPSILON)
    return (center * inv_std, inv_std, mean)


def norm_back(normed, inv_std, grad_in):
    return inv_std * (
        grad_in
        - jnp.mean(grad_in, -1, keepdims=True)
        - normed * jnp.mean(grad_in * normed, -1, keepdims=True)
    )


def gelu_tanh(values):
    return (
        0.5 * values * (1.0 + jnp.tanh(GELU_COEF * (values + 0.044715 * values * values * values)))
    )


def gelu_slope(values):
    tanh_val = jnp.tanh(GELU_COEF * (values + 0.044715 * values * values * values))
    return 0.5 * (1.0 + tanh_val) + 0.5 * values * (1.0 - tanh_val * tanh_val) * GELU_COEF * (
        1.0 + 0.134145 * values * values
    )


def silu_slope(values):
    sigmoid = jax.nn.sigmoid(values)
    return sigmoid * (1.0 + values * (1.0 - sigmoid))


def after(value, *deps):
    return lax.optimization_barrier((value,) + deps)[0]


def attend_kernel(count, q_ref, bias_ref, *refs):
    kv_refs, (o_ref, l_ref) = refs[:count], refs[count:]
    keys = jnp.concatenate([r[0] for r in kv_refs], 0)
    vals = jnp.concatenate([r[1] for r in kv_refs], 0)
    bias = bias_ref[0]
    outs, logs = [], []
    for half in range(2):
        cols = slice(half * HD, (half + 1) * HD)
        query = q_ref[:, cols] * SCALE
        scores = lax.dot_general(query, keys[:, cols], NT, preferred_element_type=F32) + bias
        top = jnp.max(scores, 1, keepdims=True)
        weights = jnp.exp(scores - top)
        total = jnp.sum(weights, 1, keepdims=True)
        mixed = jnp.dot(weights.astype(BF), vals[:, cols], preferred_element_type=F32)
        outs.append((mixed / total).astype(BF))
        logs.append(jnp.broadcast_to(top + jnp.log(total), (query.shape[0], HD)))
    o_ref[...] = jnp.concatenate(outs, 1)
    l_ref[...] = jnp.concatenate(logs, 1)


def attend_back_kernel(count, q_ref, bias_ref, o_ref, g_ref, l_ref, *refs):
    kv_refs, dq_ref, out_refs = refs[:count], refs[count], refs[count + 1 :]
    keys = jnp.concatenate([r[0] for r in kv_refs], 0)
    vals = jnp.concatenate([r[1] for r in kv_refs], 0)
    bias = bias_ref[0]
    grads_q, grads_k, grads_v = [], [], []
    for half in range(2):
        cols = slice(half * HD, (half + 1) * HD)
        query = q_ref[:, cols] * SCALE
        grad = g_ref[:, cols]
        delta = jnp.sum(grad.astype(F32) * o_ref[:, cols].astype(F32), 1, keepdims=True)
        log_total = l_ref[:, half * HD : half * HD + 1]
        scores = lax.dot_general(query, keys[:, cols], NT, preferred_element_type=F32) + bias
        probs = jnp.exp(scores - log_total)
        grad_prob = lax.dot_general(grad, vals[:, cols], NT, preferred_element_type=F32)
        grad_scores = (probs * (grad_prob - delta)).astype(BF)
        grads_q.append(
            (jnp.dot(grad_scores, keys[:, cols], preferred_element_type=F32) * SCALE).astype(BF)
        )
        grads_k.append(lax.dot_general(grad_scores, query, TN, preferred_element_type=F32))
        grads_v.append(
            lax.dot_general(probs.astype(BF), grad, TN, preferred_element_type=F32)
        )
    dq_ref[...] = jnp.concatenate(grads_q, 1)
    grad_k = jnp.concatenate(grads_k, 1).astype(BF)
    grad_v = jnp.concatenate(grads_v, 1).astype(BF)
    rows = q_ref.shape[0]
    for at in range(count):
        out_refs[at][0] = grad_k[at * rows : (at + 1) * rows]
        out_refs[at][1] = grad_v[at * rows : (at + 1) * rows]


def attention_specs(slots, rows, count):
    row_spec = pl.BlockSpec((rows, PAIR), lambda s, h: (s, h))
    bias_spec = pl.BlockSpec((1, 1, count * rows), lambda s, h: (s, 0, 0))
    kv_spec = pl.BlockSpec((2, rows, PAIR), lambda s, h: (0, s, h))
    return row_spec, bias_spec, kv_spec


def attend(query, bias, pieces):
    slots, count = bias.shape[0], len(pieces)
    rows = query.shape[0] // slots
    row_spec, bias_spec, kv_spec = attention_specs(slots, rows, count)
    return pl.pallas_call(
        partial(attend_kernel, count),
        grid=(slots, query.shape[1] // PAIR),
        in_specs=[row_spec, bias_spec] + [kv_spec] * count,
        out_specs=[row_spec, row_spec],
        out_shape=[
            jax.ShapeDtypeStruct(query.shape, BF),
            jax.ShapeDtypeStruct(query.shape, F32),
        ],
        name="attend",
    )(query, bias, *pieces)


def attend_back(query, bias, mixed, grad, log_total, pieces):
    slots, count = bias.shape[0], len(pieces)
    rows = query.shape[0] // slots
    row_spec, bias_spec, kv_spec = attention_specs(slots, rows, count)
    return pl.pallas_call(
        partial(attend_back_kernel, count),
        grid=(slots, query.shape[1] // PAIR),
        in_specs=[row_spec, bias_spec, row_spec, row_spec, row_spec] + [kv_spec] * count,
        out_specs=[row_spec] + [kv_spec] * count,
        out_shape=[jax.ShapeDtypeStruct(query.shape, BF)]
        + [jax.ShapeDtypeStruct(pieces[0].shape, BF)] * count,
        name="attend_back",
    )(query, bias, mixed, grad, log_total, *pieces)


def body(
    sizes,
    image_tokens,
    text_tokens,
    conditioning,
    seq_table,
    image_len,
    text_len,
    mod_weight,
    mod_bias,
    qkv_weight,
    qkv_bias,
    out_weight,
    out_bias,
    fc1_weight,
    fc1_bias,
    fc2_weight,
    fc2_bias,
    image_cot,
    text_cot,
):
    n_shard, n_ctx, n_tp = sizes
    group = image_tokens.shape[0]
    n_img, n_txt = image_tokens.shape[1], text_tokens.shape[1]
    rows = n_img + n_txt
    cols = image_tokens.shape[2]
    heads = cols // HD
    width = conditioning.shape[1]
    hidden_cols = fc1_weight.shape[2]
    owned_rows = mod_weight.shape[1]
    my_shard, my_ctx, my_tp = (
        lax.axis_index("shard"),
        lax.axis_index("ctx"),
        lax.axis_index("tp"),
    )
    row_begin = lax.axis_index(("shard", "ctx", "tp")) * owned_rows
    owner = lax.axis_index(("shard", "ctx"))
    n_owner = n_shard * n_ctx
    first_slot = my_shard * group

    def rotate(value, axis, size, step):
        return lax.ppermute(value, axis, [(i, (i + step) % size) for i in range(size)])

    def flip(value, bit):
        return lax.ppermute(value, "ctx", [(i, i ^ bit) for i in range(n_ctx)])

    def own_cols(value):
        return lax.dynamic_slice_in_dim(value, my_tp * cols, cols, value.ndim - 1)

    def pack(parts):
        return jnp.concatenate(parts, 1)

    def split(value):
        return (value[:, :n_img], value[:, n_img:])

    def gather_tp(value):
        wide = jnp.zeros(value.shape[:-1] + (width,), value.dtype)
        lead = (0,) * (value.ndim - 1)
        wide = lax.dynamic_update_slice(wide, value, lead + (my_tp * cols,))
        for step in (2, 1, 3):
            piece = rotate(value, "tp", n_tp, step)
            source = lax.rem(my_tp + n_tp - step, n_tp)
            wide = lax.dynamic_update_slice(wide, piece, lead + (source * cols,))
        return wide

    def scatter_tp(parts):
        packed = pack([p.astype(BF) for p in parts])
        total = own_cols(packed).astype(F32)
        for step in (2, 1, 3):
            target = lax.rem(my_tp + step, n_tp)
            piece = lax.dynamic_slice_in_dim(packed, target * cols, cols, 2)
            total = total + rotate(piece, "tp", n_tp, step).astype(F32)
        return total

    def sum_ctx(value):
        value = value + flip(value, 1)
        return value + flip(value, 2)

    def sum_tp(value):
        total = value
        for step in range(1, n_tp):
            total = total + rotate(value, "tp", n_tp, step)
        return total

    flat_qkv = qkv_weight.reshape(2, qkv_weight.shape[1], 3 * cols)
    w_qkv, w_out, w_fc1, w_fc2 = (
        lax.all_gather(w, ("shard", "ctx"), axis=1, tiled=True)
        for w in (flat_qkv, out_weight, fc1_weight, fc2_weight)
    )

    tokens = pack([image_tokens, text_tokens])
    wide_in = gather_tp(tokens)

    cond_rows = jnp.take(conditioning, seq_table, axis=0).astype(F32)
    cond_act = jax.nn.silu(cond_rows)
    act_part = lax.dynamic_slice_in_dim(cond_act, row_begin, owned_rows, 1)
    mod_local = mod_weight.astype(F32)
    mod_term = jnp.einsum("sr,xrke->sxke", act_part, mod_local, precision=PRECISE)
    bias_wide = lax.dynamic_update_slice(
        jnp.zeros(mod_bias.shape[:2] + (width,), F32), mod_bias.astype(F32), (0, 0, row_begin)
    )
    mod_term = (mod_term + bias_wide[None]).reshape(n_shard, group * 12, width)
    bias_flat = jnp.concatenate(
        [b.reshape(-1) for b in (qkv_bias, out_bias, fc1_bias, fc2_bias)]
    ).astype(F32)
    bias_rows = lax.dynamic_update_slice(
        jnp.zeros((n_owner, bias_flat.shape[0]), F32), bias_flat[None], (owner, 0)
    ).reshape(-1, width)

    def mod_message(which):
        return jnp.concatenate(
            [lax.dynamic_index_in_dim(mod_term, which, 0, keepdims=False), bias_rows], 0
        )

    message = mod_message(my_shard)
    for step in range(1, n_shard):
        message = message + rotate(
            mod_message(lax.rem(my_shard + step, n_shard)), "shard", n_shard, step
        )
    message = sum_ctx(message)
    mod_here = sum_tp(message[: group * 12]).reshape(group, 2, 6, width)
    gate_cols = own_cols(mod_here)
    bias_all = message[group * 12 :].reshape(n_owner, -1)
    bias_parts, begin = [], 0
    for b in (qkv_bias, out_bias, fc1_bias, fc2_bias):
        part = bias_all[:, begin : begin + b.size].reshape((n_owner,) + b.shape)
        begin += b.size
        part = jnp.moveaxis(part, 0, -2)
        bias_parts.append(part.reshape(b.shape[:-1] + (HD,)))
    b_qkv = bias_parts[0].reshape(2, 2, cols)
    bias_three = jnp.concatenate([b_qkv[:, 0], jnp.zeros((2, cols), F32), b_qkv[:, 1]], 1)
    b_out = bias_parts[1].reshape(2, cols)
    b_fc1 = bias_parts[2].reshape(2, hidden_cols)
    b_fc2 = bias_parts[3].reshape(2, cols)

    piece_ctx = [my_ctx, my_ctx ^ 1, my_ctx ^ 2, my_ctx ^ 3]
    here = lambda a: lax.dynamic_slice_in_dim(a, first_slot, group, 0)[:, None]
    image_here, text_here = here(image_len), here(text_len)
    valid = []
    for at in piece_ctx:
        valid.append(at * n_img + jnp.arange(n_img)[None] < image_here)
        valid.append(at * n_txt + jnp.arange(n_txt)[None] < text_here)
    key_bias = jnp.where(jnp.concatenate(valid, 1), 0.0, NEG_LARGE).astype(F32)[:, None]

    cot_wide = gather_tp(after(pack([image_cot, text_cot]), wide_in))

    def mods(which):
        return lambda stream: mod_here[:, stream, which, None]

    shift1, scale1, _, shift2, scale2, _ = (mods(j) for j in range(6))
    gates1 = [gate_cols[:, s, 2, None] for s in range(2)]
    gates2 = [gate_cols[:, s, 5, None] for s in range(2)]

    def dot(spec, a, b):
        return jnp.einsum(spec, a, b, preferred_element_type=F32)

    normed_one, inv_one, mean_one, hidden_one, packed = ([], [], [], [], [])
    for stream, values in enumerate(split(wide_in)):
        normed, inv_std, mean = layer_norm(values.astype(F32))
        hidden = (normed * (1.0 + scale1(stream)) + shift1(stream)).astype(BF)
        normed_one.append(normed)
        inv_one.append(inv_std)
        mean_one.append(mean)
        hidden_one.append(hidden)
        packed.append((dot("snd,dh->snh", hidden, w_qkv[stream]) + bias_three[stream]).astype(BF))
    packed = pack(packed).reshape(group * rows, 3 * cols)
    query = packed[:, :cols]
    kv_own = jnp.stack([packed[:, cols : 2 * cols], packed[:, 2 * cols :]], 0)
    kv_x = flip(kv_own, 2)
    kv_core = flip(kv_own, 1)
    kv_xcore = flip(kv_x, 1)
    pieces = (kv_own, kv_core, kv_x, kv_xcore)
    mixed, log_total = attend(query, key_bias, pieces)
    mixed_tok = split(mixed.reshape(group, rows, cols))
    attn = scatter_tp([dot("snh,oh->sno", mixed_tok[s], w_out[s]) for s in range(2)])
    branch_one, resid, sent = ([], [], [])
    inputs = (image_tokens, text_tokens)
    for stream, values in enumerate(split(attn)):
        branch = values + b_out[stream]
        branch_one.append(branch)
        resid.append(inputs[stream].astype(F32) + gates1[stream] * branch)
        sent.append((resid[stream] - mean_one[stream]).astype(BF))
    wide_resid = gather_tp(pack(sent))

    normed_two, inv_two, hidden_two, pre_act, act_two = ([], [], [], [], [])
    for stream, values in enumerate(split(wide_resid)):
        normed, inv_std, _ = layer_norm(values.astype(F32))
        hidden = (normed * (1.0 + scale2(stream)) + shift2(stream)).astype(BF)
        pre_values = dot("snd,df->snf", hidden, w_fc1[stream]) + b_fc1[stream]
        normed_two.append(normed)
        inv_two.append(inv_std)
        hidden_two.append(hidden)
        pre_act.append(pre_values)
        act_two.append(gelu_tanh(pre_values).astype(BF))
    grad_two_wide = [
        (c.astype(F32) * mod_here[:, s, 5, None]).astype(BF) for s, c in enumerate(split(cot_wide))
    ]
    fc1_bias_sums, grad_act_half, grad_hidden_two, back_two = ([], [], [], [])
    for stream in range(2):
        grad_act = dot("sno,of->snf", grad_two_wide[stream], w_fc2[stream]) * gelu_slope(
            pre_act[stream]
        )
        fc1_bias_sums.append(jnp.sum(grad_act, (0, 1)))
        grad_act_half.append(grad_act.astype(BF))
        grad_hidden = dot("snf,df->snd", grad_act_half[stream], w_fc1[stream])
        grad_hidden_two.append(grad_hidden)
        back_two.append(
            norm_back(
                normed_two[stream], inv_two[stream], grad_hidden * (1.0 + scale2(stream))
            )
        )
    back_two_sum = split(scatter_tp(back_two))
    fc2_grads = [dot("sno,snf->of", grad_two_wide[s], act_two[s]).astype(BF) for s in range(2)]
    fc1_grads = [dot("snd,snf->df", hidden_two[s], grad_act_half[s]).astype(BF) for s in range(2)]
    cots = [c.astype(F32) for c in (image_cot, text_cot)]
    grad_resid = [cots[s] + back_two_sum[s] for s in range(2)]
    grad_one = [grad_resid[s] * gates1[s] for s in range(2)]
    grad_one_wide = gather_tp(pack([g.astype(BF) for g in grad_one]))

    out_grads, grad_mixed = ([], [])
    for stream, values in enumerate(split(grad_one_wide)):
        grad_mixed.append(dot("sno,oh->snh", values, w_out[stream]).astype(BF))
        out_grads.append(dot("sno,snh->oh", values, mixed_tok[stream]).astype(BF))
    grad_mixed = pack(grad_mixed).reshape(group * rows, cols)
    grad_query, *grad_kv = attend_back(query, key_bias, mixed, grad_mixed, log_total, pieces)
    grad_own, grad_core, grad_x, grad_xcore = grad_kv
    from_core = flip(jnp.stack([grad_core, grad_xcore], 0), 1)
    sum_x = (grad_x.astype(F32) + from_core[1].astype(F32)).astype(BF)
    from_x = flip(sum_x, 2)
    grad_key_value = (
        grad_own.astype(F32) + from_core[0].astype(F32) + from_x.astype(F32)
    ).astype(BF)

    mlp_parts = [dot("snf,of->sno", act_two[s], w_fc2[s]) for s in range(2)]
    mlp_sum = split(scatter_tp(after(tuple(mlp_parts), grad_one_wide)))
    branch_two = [mlp_sum[s] + b_fc2[s] for s in range(2)]
    outputs = [(resid[s] + gates2[s] * branch_two[s]).astype(BF) for s in range(2)]

    grad_packed = jnp.concatenate([grad_query, grad_key_value[0], grad_key_value[1]], 1)
    grad_tok = split(grad_packed.reshape(group, rows, 3 * cols))
    qkv_grads, qkv_bias_sums, grad_hidden_one, back_one = ([], [], [], [])
    for stream in range(2):
        qkv_grads.append(dot("snd,snh->dh", hidden_one[stream], grad_tok[stream]).astype(BF))
        bias_sum = jnp.sum(grad_tok[stream], (0, 1), dtype=F32)
        qkv_bias_sums.append(jnp.concatenate([bias_sum[:cols], bias_sum[2 * cols :]]))
        grad_hidden = dot("snh,dh->snd", grad_tok[stream], w_qkv[stream])
        grad_hidden_one.append(grad_hidden)
        back_one.append(
            norm_back(
                normed_one[stream], inv_one[stream], grad_hidden * (1.0 + scale1(stream))
            )
        )
    back_one_sum = split(scatter_tp(back_one))
    input_grads = [grad_resid[s] + back_one_sum[s] for s in range(2)]

    def place_cols(values):
        return lax.dynamic_update_slice(
            jnp.zeros((group, width), F32), values, (0, my_tp * cols)
        )

    def all_slots(pieces_of, extra):
        mod_rows = jnp.stack([jnp.stack(p, 1) for p in pieces_of], 1)
        count = mod_rows.shape[2]
        mod_rows = mod_rows.reshape(-1, width)
        lead = mod_rows.shape[0]
        both = sum_ctx(jnp.concatenate([mod_rows, extra.reshape(-1, width)], 0))
        both = jnp.concatenate([sum_tp(both[:lead]), both[lead:]], 0)
        slots = jnp.zeros((n_shard, lead, width), F32)
        slots = lax.dynamic_update_slice(slots, both[None, :lead], (my_shard, 0, 0))
        sums = both[lead:]
        for step in range(1, n_shard):
            other = rotate(both, "shard", n_shard, step)
            source = lax.rem(my_shard + n_shard - step, n_shard)
            slots = lax.dynamic_update_slice(slots, other[None, :lead], (source, 0, 0))
            sums = sums + other[lead:]
        return slots.reshape(n_shard * group, 2, count, width), sums

    grad_one_sums = jnp.concatenate([jnp.sum(g, (0, 1)) for g in grad_one])
    grad_two_sums = jnp.concatenate(
        [jnp.sum(cots[s] * gates2[s], (0, 1)) for s in range(2)]
    )
    pad = jnp.zeros((-2 * (grad_one_sums.size + hidden_cols)) % width, F32)
    early = jnp.concatenate([grad_one_sums, grad_two_sums] + fc1_bias_sums + [pad])
    late_mods, early_sums = all_slots(
        [
            [
                place_cols(jnp.sum(grad_resid[s] * branch_one[s], 1)),
                jnp.sum(grad_hidden_two[s], 1),
                jnp.sum(grad_hidden_two[s] * normed_two[s], 1),
                place_cols(jnp.sum(cots[s] * branch_two[s], 1)),
            ]
            for s in range(2)
        ],
        early,
    )
    late = jnp.concatenate(qkv_bias_sums)
    late = jnp.concatenate([late, jnp.zeros((-late.size) % width, F32)])
    first_mods, late_sums = all_slots(
        [
            [jnp.sum(grad_hidden_one[s], 1), jnp.sum(grad_hidden_one[s] * normed_one[s], 1)]
            for s in range(2)
        ],
        late,
    )
    grad_mod = jnp.concatenate([first_mods, late_mods], 2)
    mod_weight_grad = jnp.einsum("sr,sxke->xrke", act_part, grad_mod, precision=PRECISE)
    mod_bias_grad = lax.dynamic_slice_in_dim(jnp.sum(grad_mod, 0), row_begin, owned_rows, 2)
    act_grad = jnp.einsum("sxke,xrke->sr", grad_mod, mod_local, precision=PRECISE)
    slot_grad = act_grad * silu_slope(
        lax.dynamic_slice_in_dim(cond_rows, row_begin, owned_rows, 1)
    )
    cond_grad = jnp.zeros((conditioning.shape[0], owned_rows), F32).at[seq_table].add(slot_grad)

    def own_bias(flat, like):
        full = flat.reshape(like.shape[:-1] + (HD,))
        return lax.dynamic_slice_in_dim(
            full, owner * like.shape[-1], like.shape[-1], like.ndim - 1
        )

    early_sums = early_sums.reshape(-1)
    half = 2 * cols
    qkv_bias_grad = own_bias(late_sums.reshape(-1)[: 2 * half], qkv_bias)
    out_bias_grad = own_bias(early_sums[:half], out_bias)
    fc2_bias_grad = own_bias(early_sums[half : 2 * half], fc2_bias)
    fc1_bias_grad = own_bias(early_sums[2 * half : 2 * half + 2 * hidden_cols], fc1_bias)

    def owned(grads):
        total = lax.psum_scatter(
            jnp.stack(grads, 0), ("shard", "ctx"), scatter_dimension=1, tiled=True
        )
        return total.astype(F32)

    fc2_weight_grad = owned(fc2_grads)
    fc1_weight_grad = owned(fc1_grads)
    out_weight_grad = owned(out_grads)
    qkv_weight_grad = owned(qkv_grads).reshape(qkv_weight.shape)
    return (
        outputs[0],
        outputs[1],
        input_grads[0],
        input_grads[1],
        cond_grad,
        mod_weight_grad,
        mod_bias_grad,
        qkv_weight_grad,
        qkv_bias_grad,
        out_weight_grad,
        out_bias_grad,
        fc1_weight_grad,
        fc1_bias_grad,
        fc2_weight_grad,
        fc2_bias_grad,
    )


def solution(mesh):
    sizes = (mesh.shape["shard"], mesh.shape["ctx"], mesh.shape["tp"])
    token = P("shard", "ctx", "tp")
    everywhere = ("shard", "ctx", "tp")
    spread = ("shard", "ctx")
    mod_w, mod_b = P(None, everywhere, None, None), P(None, None, everywhere)
    qkv_w, qkv_b = P(None, spread, None, "tp"), P(None, None, "tp", spread)
    mat, vec = P(None, spread, "tp"), P(None, "tp", spread)
    return jax.shard_map(
        partial(body, sizes),
        mesh=mesh,
        in_specs=(token, token, P(), P(), P(), P(), mod_w, mod_b, qkv_w, qkv_b)
        + (mat, vec, mat, vec, mat, vec, token, token),
        out_specs=(token, token, token, token, P(None, everywhere), mod_w, mod_b, qkv_w, qkv_b)
        + (mat, vec, mat, vec, mat, vec),
        check_vma=False,
    )
```
